1024 devices in a mesh: pipe: 16 (over y, core), ctx: 64 (over z, x).
Axes of the slice: x: 4, y: 8, z: 16, core: 2. Of those that a mesh axis runs over, the one named last changes fastest.
Arguments:
- incoming: bfloat16 [16, 8192, 1024], P('pipe', 'ctx'), may hold values from -6 to 6
- fresh: bfloat16 [8192, 1024], P('ctx'), may hold values from -6 to 6
- w_uvqk: bfloat16 [16, 1024, 2048], P('pipe'), may hold values from -0.1875 to 0.1875
- w_out: bfloat16 [16, 512, 1024], P('pipe'), may hold values from -0.25 to 0.25
- cache_kv: bfloat16 [16, 2, 1024, 1024], P('pipe', None, 'ctx'), may hold values from -6 to 6
- rows_user: int32 [17, 8192], P(None, 'ctx'), may hold values from 0 to 3, never falling along the last dimension, each value on 1 to 4096 neighbouring positions
- cache_len: int32 [17, 4], replicated, may hold values from 1 to 512, 1024 in all within a row
Outputs:
- section_out: bfloat16 [16, 2, 8192, 1024], P('pipe', None, 'ctx')
The draws below stay inside these ranges and needn't reach their ends.
Inputs may be any that keep to these rules, and one draw needn't show every extreme that they name: `rows_user`: each micro-batch's row users never fall along the events; every user has at least one event. `cache_len`: each micro-batch's row sums to 1024.
All inputs are finite; a program needn't handle non-finite values.
Results may differ from the reference program's by a relative error of at most 0.0085.
Values may be sent and summed in bfloat16 or wider, within the bound.
No kernel may reach another device: no remote copies, remote signals or barrier semaphores. Data moves between devices by JAX's collectives and lax.ppermute only.
A program may use at most 32 MiB of HBM per device.

```python
import math
import jax
import jax.numpy as jnp
import numpy as np
from jax import lax

D = 1024
HEADS = 4
HD = 128
HW = 512
TOK_DEV = 128
USERS = 4
STEPS = 2
SECTIONS = 16
BATCHES = 17
TOKENS = 8192
CACHE = 1024
N_CTX = 64


def block_levels(key, shape, cuts, smallest, top_value):
    loudness = 1.0
    for axis_at, shards_of in cuts:
        steps = jax.random.uniform(jax.random.fold_in(jax.random.fold_in(key, 6), axis_at), (shards_of,), jnp.float32, smallest / len(cuts), top_value / len(cuts))
        loudness = loudness * jnp.repeat(jnp.exp(steps), shape[axis_at] // shards_of).reshape((-1,) + (1,) * (len(shape) - 1 - axis_at))
    return loudness


def split_up(count, total, limit, skew):
    weights = [(1 << 20) // math.isqrt(standing ** skew) + 1 for standing in range(2, count + 1)]
    spare, counts = total - limit - (count - 1), [1] * (count - 1)
    while spare > 0:
        candidates = [i for i in range(count - 1) if counts[i] < limit]
        pool, budget = sum([weights[i] for i in candidates]), spare
        for i in candidates:
            addition = min(limit - counts[i], max(1, budget * weights[i] // pool), spare)
            counts[i] = counts[i] + addition
            spare = spare - addition
    return np.array([limit] + counts)


def uneven(key, count, total, limit, lean):
    if count == 2:
        one = jax.random.randint(key, (), max(1, total - limit), min(limit, total - 1) + 1)
        return jnp.stack([one, total - one])
    sizes = jnp.asarray(split_up(count, total, limit, lean), jnp.int32)
    twos = (count - 1) // 2
    donor, sink = sizes[1:1 + 2 * twos:2], sizes[2:2 + 2 * twos:2]
    slack = jnp.minimum(donor - 1, limit - sink)
    moved = jax.random.randint(jax.random.fold_in(key, 1), (twos,), 0, 1 << 20) % (slack + 1)
    sizes = sizes.at[1:1 + 2 * twos:2].set(donor - moved).at[2:2 + 2 * twos:2].set(sink + moved)
    return sizes[jax.random.permutation(jax.random.fold_in(key, 2), count)]


def bell_draw(own_key, extent, scale, reach, split=(), held_as=jnp.bfloat16):
    array = jax.random.normal(own_key, extent, jnp.float32) * scale
    if len(split) > 0:
        array = block_levels(own_key, extent, split, -0.22, 0.18) * array
    return jnp.clip(array, min=-reach, max=reach).astype(held_as)


def setup_inputs(seed: int = 0) -> dict:
    seeds = jax.random.split(jax.random.key(seed), 8)
    return {
        "incoming": bell_draw(seeds[0], (SECTIONS, TOKENS, D), 1.0, 6.0, ((0, 16), (1, 64))),
        "fresh": bell_draw(seeds[1], (TOKENS, D), 1.0, 6.0, ((0, 64),)),
        "w_uvqk": bell_draw(seeds[2], (SECTIONS, D, 4 * HW), D ** -0.5, 0.1875, ((0, 16),)),
        "w_out": bell_draw(seeds[3], (SECTIONS, HW, D), HW ** -0.5, 0.25, ((0, 16),)),
        "cache_kv": bell_draw(seeds[4], (SECTIONS, STEPS, CACHE, 2 * HW), 1.0, 6.0, ((0, 16), (2, 64))),
        "rows_user": jax.vmap(lambda own: jnp.searchsorted(jnp.cumsum(uneven(own, USERS, TOKENS, TOKENS // 2, 2)), jnp.arange(TOKENS), side="right"))(jax.random.split(seeds[5], BATCHES)).reshape((BATCHES, TOKENS)).astype(jnp.int32),
        "cache_len": jax.vmap(lambda own: uneven(own, USERS, CACHE, CACHE // 2, 1))(jax.random.split(seeds[6], BATCHES)).reshape((BATCHES, USERS)).astype(jnp.int32),
    }


def normalize(values):
    center = lax.optimization_barrier(jnp.mean(values, axis=-1, keepdims=True))
    shifted = values - center
    spread = lax.optimization_barrier(jnp.mean(shifted * shifted, axis=-1, keepdims=True))
    return shifted * lax.rsqrt(spread + 1e-06)

def owners(positions, lengths):
    bounds = jnp.cumsum(lengths.astype(jnp.int32)).astype(jnp.int32)
    return lax.optimization_barrier(jnp.sum((positions[:, None] >= bounds[None, :-1]).astype(jnp.int32), axis=1)).astype(jnp.int32)

def layer(inputs, w_in, w_back, cache_rows, users, lengths):
    width = w_back.shape[0]
    scale = HD ** (-0.5)
    normed = normalize(inputs.astype(jnp.float32)).astype(jnp.bfloat16)
    projected = jax.nn.silu(jnp.dot(normed, w_in, preferred_element_type=jnp.float32)).astype(jnp.bfloat16)
    gate_u = projected[:, :width]
    cache_user = owners(jnp.arange(CACHE, dtype=jnp.int32), lengths)
    cache_keys = cache_rows[:, :width].astype(jnp.float32).reshape(CACHE, HEADS, HD)
    cache_values = cache_rows[:, width:].astype(jnp.float32).reshape(CACHE, HEADS, HD)
    row_index = jnp.arange(TOK_DEV, dtype=jnp.int32)
    causal = row_index[None, :] <= row_index[:, None]

    def block_term(packed):
        block_q, block_k, block_v, block_users = packed
        query = block_q.astype(jnp.float32).reshape(TOK_DEV, HEADS, HD)
        own_keys = block_k.astype(jnp.float32).reshape(TOK_DEV, HEADS, HD)
        own_values = block_v.astype(jnp.float32).reshape(TOK_DEV, HEADS, HD)
        scores = jnp.einsum('thd,chd->htc', query, cache_keys)
        allowed = (block_users[:, None] == cache_user[None, :]).astype(jnp.float32)
        weights = (jax.nn.silu(scale * scores) * allowed[None]).astype(jnp.bfloat16).astype(jnp.float32)
        total = jnp.einsum('htc,chd->thd', weights, cache_values)
        local_scores = jnp.einsum('thd,rhd->htr', query, own_keys)
        local_allowed = (causal & (block_users[:, None] == block_users[None, :])).astype(jnp.float32)
        local_weights = (jax.nn.silu(scale * local_scores) * local_allowed[None]).astype(jnp.bfloat16).astype(jnp.float32)
        total = total + jnp.einsum('htr,rhd->thd', local_weights, own_values)
        return total.reshape(TOK_DEV, width)
    packed = (projected[:, width:2 * width].reshape(N_CTX, TOK_DEV, width), projected[:, 2 * width:3 * width].reshape(N_CTX, TOK_DEV, width), projected[:, 3 * width:].reshape(N_CTX, TOK_DEV, width), users.reshape(N_CTX, TOK_DEV))
    attn = lax.map(block_term, packed).reshape(TOKENS, width)
    mixed = (normalize(attn) * gate_u.astype(jnp.float32)).astype(jnp.bfloat16)
    return (jnp.dot(mixed, w_back, preferred_element_type=jnp.float32) + inputs.astype(jnp.float32)).astype(jnp.bfloat16)

def reference(incoming, fresh, w_uvqk, w_out, cache_kv, rows_user, cache_len):
    first = []
    for section in range(SECTIONS):
        batch = SECTIONS - 1 - section
        first.append(layer(incoming[section], w_uvqk[section], w_out[section], cache_kv[section, 0], rows_user[batch], cache_len[batch]))
    second = []
    for section in range(SECTIONS):
        batch = SECTIONS - section
        source = fresh if section == 0 else first[section - 1]
        second.append(layer(source, w_uvqk[section], w_out[section], cache_kv[section, 1], rows_user[batch], cache_len[batch]))
    return jnp.stack([jnp.stack([first[section], second[section]]) for section in range(SECTIONS)])
```

```python
import functools

import jax
import jax.numpy as jnp
from jax import lax
from jax.experimental import pallas as pl
from jax.experimental.pallas import tpu as pltpu
from jax.sharding import PartitionSpec as P


HEADS = 4
HD = 128
HW = HEADS * HD
STEPS = 2
NX = 4
NZ = 16
USERS = 4
SHARE = 16
EVENS = [[z * NX + x for z in range(p, NZ, 2)] for p in range(2) for x in range(NX)]
SQUARES = [[(2 * i + p) * NX + x for p in range(2) for x in range(NX)] for i in range(NZ // 2)]
PAIR = [(c, (c // NX ^ 1) * NX + c % NX) for c in range(NX * NZ)]
SPAN = SHARE * NZ // 2


def along_x(distance):
    return [(c, (c // NX) * NX + (c % NX + distance) % NX) for c in range(NX * NZ)]


def half_silu(half):
    return half + half * jnp.tanh(half)


def normalize(values):
    center = jnp.mean(values, axis=-1, keepdims=True)
    shifted = values - center
    spread = jnp.mean(shifted * shifted, axis=-1, keepdims=True)
    return shifted * lax.rsqrt(spread + 1e-06)


def dot_t(a, b):
    return lax.dot_general(a, b, (((1,), (1,)), ((), ())), preferred_element_type=jnp.float32)


def user_columns(users_ref, step):
    batch = lax.axis_size("pipe") - 1 - lax.axis_index("pipe") + step
    row = users_ref[pl.ds(batch, 1), :].astype(jnp.float32)
    square = jnp.broadcast_to(row, (row.shape[1], row.shape[1]))
    return square, square.T


def current_of(refs, step):
    if step == 0:
        return refs[0][...]
    passed, fresh = refs
    return jnp.where(lax.axis_index("pipe") == 0, fresh[...], passed[...])


def project_kernel(step, n_x, *refs):
    x_refs, (w_ref, users_ref, uq_ref, attn_ref, normed, keys) = refs[:n_x], refs[n_x:]
    part = pl.program_id(0)

    @pl.when(part == 0)
    def _():
        x = current_of(x_refs, step).astype(jnp.float32)
        normed[...] = normalize(x).astype(jnp.bfloat16)

    def projected():
        wide = jnp.dot(normed[...], w_ref[...], preferred_element_type=jnp.float32)
        return half_silu(0.5 * wide).astype(jnp.bfloat16)

    @pl.when(part == 0)
    def _():
        uq_ref[:, HW:] = projected()

    @pl.when(part == 1)
    def _():
        keys[...] = projected()

    @pl.when(part == 2)
    def _():
        values = projected()
        rows, columns = user_columns(users_ref, step)
        t = lax.broadcasted_iota(jnp.int32, rows.shape, 0)
        n = lax.broadcasted_iota(jnp.int32, rows.shape, 1)
        allowed = (rows == columns) & (n <= t)
        for h in range(HEADS):
            s = slice(h * HD, (h + 1) * HD)
            scores = dot_t(uq_ref[:, HW + h * HD : HW + (h + 1) * HD], keys[:, s])
            weights = jnp.where(allowed, half_silu((0.5 * HD**-0.5) * scores), 0.0)
            attn_ref[:, s] = jnp.dot(
                weights.astype(jnp.bfloat16), values[:, s], preferred_element_type=jnp.float32
            )

    @pl.when(part == 3)
    def _():
        uq_ref[:, :HW] = projected()


def attend_kernel(step, n_x, sizes, *refs):
    count = len(sizes)
    x_refs, refs = refs[:n_x], refs[n_x:]
    u_ref, q_ref, local_ref, w_ref, users_ref, len_ref = refs[:6]
    key_refs, value_refs = refs[6 : 6 + count], refs[6 + count : 6 + 2 * count]
    rest = refs[6 + 2 * count :]
    if step > 0:
        first_ref, out_ref, attn, masks = rest
    else:
        out_ref, attn, masks = rest
    head = pl.program_id(0)
    place = lax.axis_index("ctx")
    x0, z0 = place % NX, place // NX

    @pl.when(head == 0)
    def _():
        batch = lax.axis_size("pipe") - 1 - lax.axis_index("pipe") + step
        bounds, total = [], 0
        for g in range(USERS - 1):
            total = total + len_ref[batch, g]
            bounds.append(total)
        _, columns = user_columns(users_ref, step)
        n = lax.broadcasted_iota(jnp.int32, (8, SPAN), 1)
        base = (n // SHARE) * (2 * NX * SHARE) + n % SHARE
        for b in range(2 * NX):
            if step == 0:
                offset = b * SHARE
            else:
                offset = ((z0 + b) % 2) * (NX * SHARE) + ((x0 + (0, 3, 1, 2)[b // 2]) % NX) * SHARE
            position = base + offset
            owner = sum((position >= bound).astype(jnp.int32) for bound in bounds)
            row = jnp.broadcast_to(owner[:1].astype(jnp.float32), columns.shape)
            masks[:, b * SPAN : (b + 1) * SPAN] = (row == columns).astype(jnp.float32)

    queries = q_ref[...]
    total = local_ref[...]
    at = 0
    for key_ref, value_ref, size in zip(key_refs, value_refs, sizes):
        for begin in range(0, size, 2 * SPAN):
            wide = min(2 * SPAN, size - begin)
            scores = dot_t(queries, key_ref[begin : begin + wide, :])
            weights = half_silu((0.5 * HD**-0.5) * scores) * masks[:, at : at + wide]
            total = total + jnp.dot(
                weights.astype(jnp.bfloat16),
                value_ref[begin : begin + wide, :],
                preferred_element_type=jnp.float32,
            )
            at += wide
    attn[head] = total

    @pl.when(head == HEADS - 1)
    def _():
        whole = jnp.concatenate([attn[h] for h in range(HEADS)], axis=1)
        mixed = (normalize(whole) * u_ref[...].astype(jnp.float32)).astype(jnp.bfloat16)
        result = jnp.dot(mixed, w_ref[...], preferred_element_type=jnp.float32)
        result = (result + current_of(x_refs, step).astype(jnp.float32)).astype(jnp.bfloat16)
        if step > 0:
            out_ref[0] = first_ref[...]
            out_ref[1] = result
        else:
            out_ref[...] = result


def whole(shape):
    return pl.BlockSpec(shape, lambda j: (0,) * len(shape))


def project(step, x_list, w, users):
    t, d = x_list[0].shape
    return pl.pallas_call(
        functools.partial(project_kernel, step, len(x_list)),
        grid=(4,),
        in_specs=[whole((t, d)) for _ in x_list]
        + [pl.BlockSpec((d, HW), lambda j: (0, (j + 1) % 4)), whole(users.shape)],
        out_specs=[whole((t, 2 * HW)), whole((t, HW))],
        out_shape=[
            jax.ShapeDtypeStruct((t, 2 * HW), jnp.bfloat16),
            jax.ShapeDtypeStruct((t, HW), jnp.float32),
        ],
        scratch_shapes=[pltpu.VMEM((t, d), jnp.bfloat16), pltpu.VMEM((t, HW), jnp.bfloat16)],
    )(*x_list, w, users)


def attend(step, x_list, uq, local, w_back, users, lengths, rows, first=None):
    t, d = x_list[0].shape
    sizes = [r.shape[0] for r in rows]
    shape = (t, d) if step == 0 else (STEPS, t, d)
    in_specs = [whole((t, d)) for _ in x_list]
    in_specs += [
        pl.BlockSpec((t, HW), lambda j: (0, 0)),
        pl.BlockSpec((t, HD), lambda j: (0, HEADS + j)),
        pl.BlockSpec((t, HD), lambda j: (0, j)),
        whole((HW, d)),
        whole(users.shape),
        pl.BlockSpec(memory_space=pltpu.SMEM),
    ]
    in_specs += [pl.BlockSpec((size, HD), lambda j: (0, j)) for size in sizes]
    in_specs += [pl.BlockSpec((size, HD), lambda j: (0, HEADS + j)) for size in sizes]
    args = [*x_list, uq, uq, local, w_back, users, lengths, *rows, *rows]
    if step > 0:
        in_specs.append(whole((t, d)))
        args.append(first)
    return pl.pallas_call(
        functools.partial(attend_kernel, step, len(x_list), sizes),
        grid=(HEADS,),
        in_specs=in_specs,
        out_specs=whole(shape),
        out_shape=jax.ShapeDtypeStruct(shape, jnp.bfloat16),
        scratch_shapes=[
            pltpu.VMEM((HEADS, t, HD), jnp.float32),
            pltpu.VMEM((t, sum(sizes)), jnp.float32),
        ],
    )(*args)


def body(incoming, fresh, w_uvqk, w_out, cache_kv, rows_user, cache_len):
    w_in, w_back = w_uvqk[0], w_out[0]
    evens = lax.all_gather(cache_kv[0], "ctx", axis=0, tiled=False, axis_index_groups=EVENS)
    column = [evens[:, t].reshape(SPAN, 2 * HW) for t in range(STEPS)]
    other = lax.ppermute(column[1], "ctx", PAIR)
    spread = jnp.broadcast_to(column[0][None], (2 * NX, SPAN, 2 * HW))
    rows0 = lax.all_to_all(spread, "ctx", 0, 0, axis_index_groups=SQUARES)
    rows0 = rows0.reshape(2 * NX * SPAN, 2 * HW)
    mine, other, rows0 = lax.optimization_barrier((column[1], other, rows0))
    near = jnp.concatenate([mine, other], axis=0)
    from_left = lax.ppermute(near, "ctx", along_x(1))
    from_right = lax.ppermute(near, "ctx", along_x(-1))
    across = lax.ppermute(mine, "ctx", along_x(2))
    across = [across, lax.ppermute(other, "ctx", along_x(-2))]
    rows1 = [near, from_left, from_right, *across]
    uq, local = project(0, [incoming[0]], w_in, rows_user)
    first = attend(0, [incoming[0]], uq, local, w_back, rows_user, cache_len, [rows0])
    sections = lax.axis_size("pipe")
    passed = lax.ppermute(first, "pipe", [(i, i + 1) for i in range(sections - 1)])
    uq, local = project(1, [passed, fresh], w_in, rows_user)
    both = attend(1, [passed, fresh], uq, local, w_back, rows_user, cache_len, rows1, first)
    return both[None]


def solution(mesh):
    in_specs = (
        P("pipe", "ctx", None),
        P("ctx", None),
        P("pipe", None, None),
        P("pipe", None, None),
        P("pipe", None, "ctx", None),
        P(None, "ctx"),
        P(),
    )
    out_specs = P("pipe", None, "ctx", None)
    return jax.shard_map(body, mesh=mesh, in_specs=in_specs, out_specs=out_specs, check_vma=False)
```

```python
import functools

import jax
import jax.numpy as jnp
from jax import lax
from jax.experimental import pallas as pl
from jax.experimental.pallas import tpu as pltpu
from jax.sharding import PartitionSpec as P

HEADS = 4
HD = 128
HW = HEADS * HD
STEPS = 2
NX = 4
NZ = 16
USERS = 4
SHARE = 16
EVENS = [[z * NX + x for z in range(p, NZ, 2)] for p in range(2) for x in range(NX)]
SQUARES = [[(2 * i + p) * NX + x for p in range(2) for x in range(NX)] for i in range(NZ // 2)]
LINES = [[z * NX + x for x in range(NX)] for z in range(NZ)]
PAIR = [(c, (c // NX + (1 if c // NX % 2 else -1)) % NZ * NX + c % NX) for c in range(NX * NZ)]
SPAN = SHARE * NZ // 2


def half_silu(half):
    return half + half * jnp.tanh(half)


def normalize(values):
    center = jnp.mean(values, axis=-1, keepdims=True)
    shifted = values - center
    spread = jnp.mean(shifted * shifted, axis=-1, keepdims=True)
    return shifted * lax.rsqrt(spread + 1e-06)


def dot_t(a, b):
    return lax.dot_general(a, b, (((1,), (1,)), ((), ())), preferred_element_type=jnp.float32)


def user_columns(users_ref, step):
    batch = lax.axis_size("pipe") - 1 - lax.axis_index("pipe") + step
    row = users_ref[pl.ds(batch, 1), :].astype(jnp.float32)
    square = jnp.broadcast_to(row, (row.shape[1], row.shape[1]))
    return square, square.T


def current_of(refs, step):
    if step == 0:
        return refs[0][...]
    passed, fresh = refs
    return jnp.where(lax.axis_index("pipe") == 0, fresh[...], passed[...])


def project_kernel(step, n_x, *refs):
    x_refs, (w_ref, users_ref, uq_ref, attn_ref, normed, keys) = refs[:n_x], refs[n_x:]
    part = pl.program_id(0)

    @pl.when(part == 0)
    def _():
        x = current_of(x_refs, step).astype(jnp.float32)
        normed[...] = normalize(x).astype(jnp.bfloat16)

    def projected():
        wide = jnp.dot(normed[...], w_ref[...], preferred_element_type=jnp.float32)
        return half_silu(0.5 * wide).astype(jnp.bfloat16)

    @pl.when(part == 0)
    def _():
        uq_ref[:, HW:] = projected()

    @pl.when(part == 1)
    def _():
        keys[...] = projected()

    @pl.when(part == 2)
    def _():
        values = projected()
        rows, columns = user_columns(users_ref, step)
        t = lax.broadcasted_iota(jnp.int32, rows.shape, 0)
        n = lax.broadcasted_iota(jnp.int32, rows.shape, 1)
        allowed = (rows == columns) & (n <= t)
        for h in range(HEADS):
            s = slice(h * HD, (h + 1) * HD)
            scores = dot_t(uq_ref[:, HW + h * HD : HW + (h + 1) * HD], keys[:, s])
            weights = jnp.where(allowed, half_silu((0.5 * HD**-0.5) * scores), 0.0)
            attn_ref[:, s] = jnp.dot(
                weights.astype(jnp.bfloat16), values[:, s], preferred_element_type=jnp.float32
            )

    @pl.when(part == 3)
    def _():
        uq_ref[:, :HW] = projected()


def masks_kernel(users_ref, len_ref, *mask_refs):
    n = lax.broadcasted_iota(jnp.int32, (8, SPAN), 1)
    base = (n // SHARE) * (2 * NX * SHARE) + n % SHARE
    for step in range(STEPS):
        batch = lax.axis_size("pipe") - 1 - lax.axis_index("pipe") + step
        bounds, total = [], 0
        for g in range(USERS - 1):
            total = total + len_ref[batch, g]
            bounds.append(total)
        _, columns = user_columns(users_ref, step)
        for b in range(2 * NX):
            if step == 0:
                offset = b * SHARE
            else:
                offset = ((lax.axis_index("ctx") // NX + b) % 2) * (NX * SHARE) + b // 2 * SHARE
            position = base + offset
            owner = sum((position >= bound).astype(jnp.int32) for bound in bounds)
            row = jnp.broadcast_to(owner[:1].astype(jnp.float32), columns.shape)
            mask = (row == columns).astype(jnp.float32).astype(jnp.bfloat16)
            mask_refs[step][:, b * SPAN : (b + 1) * SPAN] = mask


def attend_kernel(step, n_x, sizes, *refs):
    count = len(sizes)
    x_refs, refs = refs[:n_x], refs[n_x:]
    u_ref, q_ref, local_ref, w_ref, masks = refs[:5]
    key_refs, value_refs = refs[5 : 5 + count], refs[5 + count : 5 + 2 * count]
    rest = refs[5 + 2 * count :]
    if step > 0:
        first_ref, out_ref, attn = rest
    else:
        out_ref, attn = rest
    head = pl.program_id(0)

    queries = q_ref[...]
    total = local_ref[...]
    at = 0
    for key_ref, value_ref, size in zip(key_refs, value_refs, sizes):
        for begin in range(0, size, 2 * SPAN):
            wide = min(2 * SPAN, size - begin)
            scores = dot_t(queries, key_ref[begin : begin + wide, :])
            weights = half_silu((0.5 * HD**-0.5) * scores).astype(jnp.bfloat16)
            total = total + jnp.dot(
                weights * masks[:, at : at + wide],
                value_ref[begin : begin + wide, :],
                preferred_element_type=jnp.float32,
            )
            at += wide
    attn[head] = total

    @pl.when(head == HEADS - 1)
    def _():
        whole = jnp.concatenate([attn[h] for h in range(HEADS)], axis=1)
        mixed = (normalize(whole) * u_ref[...].astype(jnp.float32)).astype(jnp.bfloat16)
        result = jnp.dot(mixed, w_ref[...], preferred_element_type=jnp.float32)
        result = (result + current_of(x_refs, step).astype(jnp.float32)).astype(jnp.bfloat16)
        if step > 0:
            out_ref[0] = first_ref[...]
            out_ref[1] = result
        else:
            out_ref[...] = result


def exchange(block, groups):
    spread = jnp.broadcast_to(block[None], (len(groups[0]), *block.shape))
    got = lax.all_to_all(spread, "ctx", 0, 0, axis_index_groups=groups)
    return got.reshape(-1, block.shape[-1])


def whole(shape):
    return pl.BlockSpec(shape, lambda j: (0,) * len(shape))


def project(step, x_list, w, users):
    t, d = x_list[0].shape
    return pl.pallas_call(
        functools.partial(project_kernel, step, len(x_list)),
        grid=(4,),
        in_specs=[whole((t, d)) for _ in x_list]
        + [pl.BlockSpec((d, HW), lambda j: (0, (j + 1) % 4)), whole(users.shape)],
        out_specs=[whole((t, 2 * HW)), whole((t, HW))],
        out_shape=[
            jax.ShapeDtypeStruct((t, 2 * HW), jnp.bfloat16),
            jax.ShapeDtypeStruct((t, HW), jnp.float32),
        ],
        scratch_shapes=[pltpu.VMEM((t, d), jnp.bfloat16), pltpu.VMEM((t, HW), jnp.bfloat16)],
    )(*x_list, w, users)


def make_masks(users, lengths):
    shape = (users.shape[1], 2 * NX * SPAN)
    return pl.pallas_call(
        masks_kernel,
        in_specs=[pl.BlockSpec(memory_space=pltpu.VMEM), pl.BlockSpec(memory_space=pltpu.SMEM)],
        out_specs=[pl.BlockSpec(memory_space=pltpu.VMEM)] * STEPS,
        out_shape=[jax.ShapeDtypeStruct(shape, jnp.bfloat16)] * STEPS,
        name="masks",
    )(users, lengths)


def attend(step, x_list, uq, local, w_back, mask, rows, first=None):
    t, d = x_list[0].shape
    sizes = [r.shape[0] for r in rows]
    shape = (t, d) if step == 0 else (STEPS, t, d)
    in_specs = [whole((t, d)) for _ in x_list]
    in_specs += [
        pl.BlockSpec((t, HW), lambda j: (0, 0)),
        pl.BlockSpec((t, HD), lambda j: (0, HEADS + j)),
        pl.BlockSpec((t, HD), lambda j: (0, j)),
        whole((HW, d)),
        whole(mask.shape),
    ]
    in_specs += [pl.BlockSpec((size, HD), lambda j: (0, j)) for size in sizes]
    in_specs += [pl.BlockSpec((size, HD), lambda j: (0, HEADS + j)) for size in sizes]
    args = [*x_list, uq, uq, local, w_back, mask, *rows, *rows]
    if step > 0:
        in_specs.append(whole((t, d)))
        args.append(first)
    return pl.pallas_call(
        functools.partial(attend_kernel, step, len(x_list), sizes),
        grid=(HEADS,),
        in_specs=in_specs,
        out_specs=whole(shape),
        out_shape=jax.ShapeDtypeStruct(shape, jnp.bfloat16),
        scratch_shapes=[
            pltpu.VMEM((HEADS, t, HD), jnp.float32),
        ],
    )(*args)


def body(incoming, fresh, w_uvqk, w_out, cache_kv, rows_user, cache_len):
    w_in, w_back = w_uvqk[0], w_out[0]
    evens = lax.all_gather(cache_kv[0], "ctx", axis=0, tiled=False, axis_index_groups=EVENS)
    column = [evens[:, t].reshape(SPAN, 2 * HW) for t in range(STEPS)]
    rows0 = exchange(column[0], SQUARES)
    other = lax.ppermute(column[1], "ctx", PAIR)
    rows1 = exchange(jnp.concatenate([column[1], other], axis=0), LINES)
    uq, local = project(0, [incoming[0]], w_in, rows_user)
    masks = make_masks(rows_user, cache_len)
    first = attend(0, [incoming[0]], uq, local, w_back, masks[0], [rows0])
    sections = lax.axis_size("pipe")
    passed = lax.ppermute(first, "pipe", [(i, i + 1) for i in range(sections - 1)])
    uq, local = project(1, [passed, fresh], w_in, rows_user)
    both = attend(1, [passed, fresh], uq, local, w_back, masks[1], [rows1], first)
    return both[None]


def solution(mesh):
    in_specs = (
        P("pipe", "ctx", None),
        P("ctx", None),
        P("pipe", None, None),
        P("pipe", None, None),
        P("pipe", None, "ctx", None),
        P(None, "ctx"),
        P(),
    )
    out_specs = P("pipe", None, "ctx", None)
    return jax.shard_map(body, mesh=mesh, in_specs=in_specs, out_specs=out_specs, check_vma=False)
```

```python
import functools

import jax
import jax.numpy as jnp
from jax import lax
from jax.experimental import pallas as pl
from jax.experimental.pallas import tpu as pltpu
from jax.sharding import PartitionSpec as P


HEADS = 4
HD = 128
HW = HEADS * HD
STEPS = 2
NX = 4
NZ = 16
USERS = 4
SHARE = 16
EVENS = [[z * NX + x for z in range(p, NZ, 2)] for p in range(2) for x in range(NX)]
SQUARES = [[(2 * i + p) * NX + x for p in range(2) for x in range(NX)] for i in range(NZ // 2)]
PAIR = [(c, (c // NX + (1 if c // NX % 2 else -1)) % NZ * NX + c % NX) for c in range(NX * NZ)]
HOPS = (0, 3, 1, 2)
SPAN = SHARE * NZ // 2


def along_x(distance):
    return [(c, (c // NX) * NX + (c % NX + distance) % NX) for c in range(NX * NZ)]


def half_silu(half):
    return half + half * jnp.tanh(half)


def normalize(values):
    center = jnp.mean(values, axis=-1, keepdims=True)
    shifted = values - center
    spread = jnp.mean(shifted * shifted, axis=-1, keepdims=True)
    return shifted * lax.rsqrt(spread + 1e-06)


def dot_t(a, b):
    return lax.dot_general(a, b, (((1,), (1,)), ((), ())), preferred_element_type=jnp.float32)


def user_columns(users_ref, step):
    batch = lax.axis_size("pipe") - 1 - lax.axis_index("pipe") + step
    row = users_ref[pl.ds(batch, 1), :].astype(jnp.float32)
    square = jnp.broadcast_to(row, (row.shape[1], row.shape[1]))
    return square, square.T


def current_of(refs, step):
    if step == 0:
        return refs[0][...]
    passed, fresh = refs
    return jnp.where(lax.axis_index("pipe") == 0, fresh[...], passed[...])


def project_kernel(step, *refs):
    passed, (w_hbm, x_ref, users_ref, uq_ref, attn_ref, w_ref, arrived) = refs[:step], refs[step:]
    x_refs = (*passed, x_ref)
    fetches = [
        pltpu.make_async_copy(
            w_hbm.at[:, pl.ds(part * HW, HW)], w_ref.at[part], arrived.at[part]
        )
        for part in range(4)
    ]
    for part in (1, 2, 3, 0):
        fetches[part].start()
    normed = normalize(current_of(x_refs, step).astype(jnp.float32)).astype(jnp.bfloat16)

    def projected(part):
        fetches[part].wait()
        wide = jnp.dot(normed, w_ref[part], preferred_element_type=jnp.float32)
        return half_silu(0.5 * wide).astype(jnp.bfloat16)

    queries, keys, values = projected(1), projected(2), projected(3)
    uq_ref[:, HW:] = queries
    rows, columns = user_columns(users_ref, step)
    t = lax.broadcasted_iota(jnp.int32, rows.shape, 0)
    n = lax.broadcasted_iota(jnp.int32, rows.shape, 1)
    allowed = (rows == columns) & (n <= t)
    for h in range(HEADS):
        s = slice(h * HD, (h + 1) * HD)
        scores = dot_t(queries[:, s], keys[:, s])
        weights = jnp.where(allowed, half_silu((0.5 * HD**-0.5) * scores), 0.0)
        attn_ref[:, s] = jnp.dot(
            weights.astype(jnp.bfloat16), values[:, s], preferred_element_type=jnp.float32
        )
    uq_ref[:, :HW] = projected(0)


def masks_kernel(step, users_ref, len_ref, mask_ref):
    batch = lax.axis_size("pipe") - 1 - lax.axis_index("pipe") + step
    lengths = len_ref[pl.ds(batch, 1), :]
    n = lax.broadcasted_iota(jnp.int32, (8, SPAN), 1)
    base = (n // SHARE) * (2 * NX * SHARE) + n % SHARE
    bounds = [lengths[:, 0:1]]
    for g in range(1, USERS - 1):
        bounds.append(bounds[-1] + lengths[:, g : g + 1])
    bounds = [jnp.broadcast_to(bound, base.shape) for bound in bounds]
    _, columns = user_columns(users_ref, step)
    for b in range(2 * NX):
        if step == 0:
            offset = b * SHARE
        else:
            x, z = lax.axis_index("ctx") % NX, lax.axis_index("ctx") // NX
            offset = (z + b) % 2 * (NX * SHARE) + (x + HOPS[b // 2]) % NX * SHARE
        position = base + offset
        owner = sum((position >= bound).astype(jnp.int32) for bound in bounds)
        row = jnp.broadcast_to(owner[:1].astype(jnp.float32), columns.shape)
        mask = (row == columns).astype(jnp.float32).astype(jnp.bfloat16)
        mask_ref[:, b * SPAN : (b + 1) * SPAN] = mask


def attend_kernel(step, sizes, *refs):
    row_refs, w_ref, refs = refs[: len(sizes)], refs[len(sizes)], refs[len(sizes) + 1 :]
    if step > 0:
        passed, uq_ref, local_ref, x_ref, mask_ref, *rest = refs
        x_refs = (passed, x_ref)
    else:
        x_ref, uq_ref, local_ref, mask_ref, *rest = refs
        x_refs = (x_ref,)
    attn = []
    for h in range(HEADS):
        key_part, value_part = slice(h * HD, (h + 1) * HD), slice(HW + h * HD, HW + (h + 1) * HD)
        queries = uq_ref[:, value_part]
        total = local_ref[:, key_part]
        at = 0
        for row_ref, size in zip(row_refs, sizes):
            for begin in range(0, size, 2 * SPAN):
                wide = min(2 * SPAN, size - begin)
                scores = dot_t(queries, row_ref[begin : begin + wide, key_part])
                weights = half_silu((0.5 * HD**-0.5) * scores).astype(jnp.bfloat16)
                total = total + jnp.dot(
                    weights * mask_ref[:, at : at + wide],
                    row_ref[begin : begin + wide, value_part],
                    preferred_element_type=jnp.float32,
                )
                at += wide
        attn.append(total)
    whole = jnp.concatenate(attn, axis=1)
    mixed = (normalize(whole) * uq_ref[:, :HW].astype(jnp.float32)).astype(jnp.bfloat16)
    result = jnp.dot(mixed, w_ref[...], preferred_element_type=jnp.float32)
    result = (result + current_of(x_refs, step).astype(jnp.float32)).astype(jnp.bfloat16)
    if step > 0:
        first_ref, out_ref = rest
        out_ref[0] = first_ref[...]
        out_ref[1] = result
    else:
        rest[0][...] = result


def exchange(block, groups):
    spread = jnp.broadcast_to(block[None], (len(groups[0]), *block.shape))
    got = lax.all_to_all(spread, "ctx", 0, 0, axis_index_groups=groups)
    return got.reshape(-1, block.shape[-1])


RESIDENT = pl.BlockSpec(memory_space=pltpu.VMEM)


def fetched_spec(value):
    return pl.BlockSpec(value.shape, lambda j: (0,) * len(value.shape))


def call(kernel, outs, kept, fetched, lean=16, stay=(), scratch=()):
    keep = not any(isinstance(out, jax.ShapeDtypeStruct) for out in outs)
    return pl.pallas_call(
        kernel,
        grid=(1,),
        in_specs=[RESIDENT for _ in kept]
        + [pl.BlockSpec(memory_space=pltpu.HBM) for _ in stay]
        + [fetched_spec(value) for value in fetched],
        out_specs=[RESIDENT if keep else fetched_spec(out) for out in outs],
        out_shape=outs,
        scratch_shapes=list(scratch),
        compiler_params=pltpu.CompilerParams(vmem_limit_bytes=lean << 20 if lean else None),
    )(*[pltpu.with_memory_space_constraint(value, pltpu.VMEM) for value in kept], *stay, *fetched)


def project(step, x_list, w, users):
    t = x_list[0].shape[0]
    kind = pltpu.VMEM if step > 0 else jax.ShapeDtypeStruct
    outs = [kind((t, 2 * HW), jnp.bfloat16), kind((t, HW), jnp.float32)]
    kernel = functools.partial(project_kernel, step)
    scratch = [pltpu.VMEM((4, w.shape[0], HW), w.dtype), pltpu.SemaphoreType.DMA((4,))]
    kept, fetched = x_list[:step], [x_list[step], users]
    return call(kernel, outs, kept, fetched, lean=60 * step, stay=[w], scratch=scratch)


def make_mask(step, users, lengths):
    outs = [jax.ShapeDtypeStruct((users.shape[1], 2 * NX * SPAN), jnp.bfloat16)]
    kernel = functools.partial(masks_kernel, step)
    return call(kernel, outs, [], [users, lengths], lean=16 * step)[0]


def attend(step, x_list, uq, local, w_back, mask, rows, first=()):
    t, d = x_list[0].shape
    sizes = [r.shape[0] for r in rows]
    kernel = functools.partial(attend_kernel, step, sizes)
    if step > 0:
        outs = [jax.ShapeDtypeStruct((STEPS, t, d), jnp.bfloat16)]
        kept = [*rows, w_back, x_list[0], uq, local]
        return call(kernel, outs, kept, [x_list[1], mask, *first])[0]
    outs = [pltpu.VMEM((t, d), jnp.bfloat16)]
    fetched = [*x_list, uq, local, mask]
    return call(kernel, outs, [*rows, w_back], fetched, lean=0)[0]


def body(incoming, fresh, w_uvqk, w_out, cache_kv, rows_user, cache_len):
    w_in, w_back = w_uvqk[0], w_out[0]
    evens = lax.all_gather(cache_kv[0], "ctx", axis=0, tiled=False, axis_index_groups=EVENS)
    column = [evens[:, t].reshape(SPAN, 2 * HW) for t in range(STEPS)]
    rows0 = exchange(column[0], SQUARES)
    other = lax.ppermute(column[1], "ctx", PAIR)
    near = jnp.concatenate([column[1], other], axis=0)
    rows1 = [near, lax.ppermute(near, "ctx", along_x(1))]
    rows1.append(lax.ppermute(near, "ctx", along_x(-1)))
    rows1.append(lax.ppermute(column[1], "ctx", along_x(2)))
    rows1.append(lax.ppermute(other, "ctx", along_x(-2)))
    uq, local = project(0, [incoming[0]], w_in, rows_user)
    mask0 = make_mask(0, rows_user, cache_len)
    mask1 = make_mask(1, rows_user, cache_len)
    first = attend(0, [incoming[0]], uq, local, w_back, mask0, [rows0])
    sections = lax.axis_size("pipe")
    passed = lax.ppermute(first, "pipe", [(i, i + 1) for i in range(sections - 1)])
    uq, local = project(1, [passed, fresh], w_in, rows_user)
    both = attend(1, [passed, fresh], uq, local, w_back, mask1, rows1, [first])
    return both[None]


def solution(mesh):
    in_specs = (
        P("pipe", "ctx", None),
        P("ctx", None),
        P("pipe", None, None),
        P("pipe", None, None),
        P("pipe", None, "ctx", None),
        P(None, "ctx"),
        P(),
    )
    out_specs = P("pipe", None, "ctx", None)
    return jax.shard_map(body, mesh=mesh, in_specs=in_specs, out_specs=out_specs, check_vma=False)
```

```python
import functools

import jax
import jax.numpy as jnp
from jax import lax
from jax.experimental import pallas as pl
from jax.experimental.pallas import tpu as pltpu
from jax.sharding import PartitionSpec as P


HEADS = 4
HD = 128
HW = HEADS * HD
STEPS = 2
NX = 4
NZ = 16
USERS = 4
SHARE = 16
EVENS = [[z * NX + x for z in range(p, NZ, 2)] for p in range(2) for x in range(NX)]
SQUARES = [[(2 * i + p) * NX + x for p in range(2) for x in range(NX)] for i in range(NZ // 2)]
PAIR = [(c, (c // NX + (1 if c // NX % 2 else -1)) % NZ * NX + c % NX) for c in range(NX * NZ)]
HOPS = (0, 3, 1, 2)
SPAN = SHARE * NZ // 2


def along_x(distance):
    return [(c, (c // NX) * NX + (c % NX + distance) % NX) for c in range(NX * NZ)]


def half_silu(half):
    return half + half * jnp.tanh(half)


def normalize(values):
    center = jnp.mean(values, axis=-1, keepdims=True)
    shifted = values - center
    spread = jnp.mean(shifted * shifted, axis=-1, keepdims=True)
    return shifted * lax.rsqrt(spread + 1e-06)


def dot_t(a, b):
    return lax.dot_general(a, b, (((1,), (1,)), ((), ())), preferred_element_type=jnp.float32)


def user_columns(users_ref, step):
    batch = lax.axis_size("pipe") - 1 - lax.axis_index("pipe") + step
    row = users_ref[pl.ds(batch, 1), :].astype(jnp.float32)
    square = jnp.broadcast_to(row, (row.shape[1], row.shape[1]))
    return square, square.T


def current_of(refs, step):
    if step == 0:
        return refs[0][...]
    passed, fresh = refs
    return jnp.where(lax.axis_index("pipe") == 0, fresh[...], passed[...])


def project_kernel(step, *refs):
    passed, (w_hbm, x_ref, users_ref, uq_ref, attn_ref, w_ref, arrived) = refs[:step], refs[step:]
    x_refs = (*passed, x_ref)
    fetches = [
        pltpu.make_async_copy(
            w_hbm.at[:, pl.ds(part * HW, HW)], w_ref.at[part], arrived.at[part]
        )
        for part in range(4)
    ]
    for part in (1, 2, 3, 0):
        fetches[part].start()
    normed = normalize(current_of(x_refs, step).astype(jnp.float32)).astype(jnp.bfloat16)

    def projected(part):
        fetches[part].wait()
        wide = jnp.dot(normed, w_ref[part], preferred_element_type=jnp.float32)
        return half_silu(0.5 * wide).astype(jnp.bfloat16)

    queries, keys, values = projected(1), projected(2), projected(3)
    uq_ref[:, HW:] = queries
    rows, columns = user_columns(users_ref, step)
    t = lax.broadcasted_iota(jnp.int32, rows.shape, 0)
    n = lax.broadcasted_iota(jnp.int32, rows.shape, 1)
    allowed = (rows == columns) & (n <= t)
    for h in range(HEADS):
        s = slice(h * HD, (h + 1) * HD)
        scores = dot_t(queries[:, s], keys[:, s])
        weights = jnp.where(allowed, half_silu((0.5 * HD**-0.5) * scores), 0.0)
        attn_ref[:, s] = jnp.dot(
            weights.astype(jnp.bfloat16), values[:, s], preferred_element_type=jnp.float32
        )
    uq_ref[:, :HW] = projected(0)


def masks_kernel(step, users_ref, len_ref, mask_ref):
    batch = lax.axis_size("pipe") - 1 - lax.axis_index("pipe") + step
    column = lax.broadcasted_iota(jnp.int32, len_ref.shape, 1) == batch
    lengths = jnp.sum(jnp.where(column, len_ref[...], 0), axis=1, keepdims=True)
    n = lax.broadcasted_iota(jnp.int32, (8, SPAN), 1)
    base = (n // SHARE) * (2 * NX * SHARE) + n % SHARE
    bounds = [lengths[0:1]]
    for g in range(1, USERS - 1):
        bounds.append(bounds[-1] + lengths[g : g + 1])
    bounds = [jnp.broadcast_to(bound, base.shape) for bound in bounds]
    _, columns = user_columns(users_ref, step)
    for b in range(2 * NX):
        if step == 0:
            offset = b * SHARE
        else:
            x, z = lax.axis_index("ctx") % NX, lax.axis_index("ctx") // NX
            offset = (z + b) % 2 * (NX * SHARE) + (x + HOPS[b // 2]) % NX * SHARE
        position = base + offset
        owner = sum((position >= bound).astype(jnp.int32) for bound in bounds)
        row = jnp.broadcast_to(owner[:1].astype(jnp.float32), columns.shape)
        mask = (row == columns).astype(jnp.float32).astype(jnp.bfloat16)
        mask_ref[:, b * SPAN : (b + 1) * SPAN] = mask


def gathered(at, uq_ref, local_ref, mask_ref, row_refs):
    attn = []
    for h in range(HEADS):
        key_part, value_part = slice(h * HD, (h + 1) * HD), slice(HW + h * HD, HW + (h + 1) * HD)
        queries = uq_ref[:, value_part]
        total = local_ref[:, key_part]
        begin_at = at
        for row_ref in row_refs:
            size = row_ref.shape[0]
            for begin in range(0, size, 2 * SPAN):
                wide = min(2 * SPAN, size - begin)
                scores = dot_t(queries, row_ref[begin : begin + wide, key_part])
                weights = half_silu((0.5 * HD**-0.5) * scores).astype(jnp.bfloat16)
                total = total + jnp.dot(
                    weights * mask_ref[:, begin_at : begin_at + wide],
                    row_ref[begin : begin + wide, value_part],
                    preferred_element_type=jnp.float32,
                )
                begin_at += wide
        attn.append(total)
    return jnp.concatenate(attn, axis=1)


def early_kernel(*refs):
    *row_refs, uq_ref, local_ref, mask_ref, out_ref = refs
    out_ref[...] = gathered(0, uq_ref, local_ref, mask_ref, row_refs)


def attend_kernel(step, at, count, *refs):
    row_refs, w_ref, refs = refs[:count], refs[count], refs[count + 1 :]
    if step > 0:
        passed, uq_ref, local_ref, x_ref, mask_ref, *rest = refs
        x_refs = (passed, x_ref)
    else:
        x_ref, uq_ref, local_ref, mask_ref, *rest = refs
        x_refs = (x_ref,)
    whole = gathered(at, uq_ref, local_ref, mask_ref, row_refs)
    mixed = (normalize(whole) * uq_ref[:, :HW].astype(jnp.float32)).astype(jnp.bfloat16)
    result = jnp.dot(mixed, w_ref[...], preferred_element_type=jnp.float32)
    result = (result + current_of(x_refs, step).astype(jnp.float32)).astype(jnp.bfloat16)
    if step > 0:
        first_ref, out_ref = rest
        out_ref[0] = first_ref[...]
        out_ref[1] = result
    else:
        rest[0][...] = result


def exchange(block, groups):
    spread = jnp.broadcast_to(block[None], (len(groups[0]), *block.shape))
    got = lax.all_to_all(spread, "ctx", 0, 0, axis_index_groups=groups)
    return got.reshape(-1, block.shape[-1])


RESIDENT = pl.BlockSpec(memory_space=pltpu.VMEM)


def fetched_spec(value):
    return pl.BlockSpec(value.shape, lambda j: (0,) * len(value.shape))


def call(kernel, outs, kept, fetched, lean=16, stay=(), scratch=()):
    keep = not any(isinstance(out, jax.ShapeDtypeStruct) for out in outs)
    return pl.pallas_call(
        kernel,
        grid=(1,),
        in_specs=[RESIDENT for _ in kept]
        + [pl.BlockSpec(memory_space=pltpu.HBM) for _ in stay]
        + [fetched_spec(value) for value in fetched],
        out_specs=[RESIDENT if keep else fetched_spec(out) for out in outs],
        out_shape=outs,
        scratch_shapes=list(scratch),
        compiler_params=pltpu.CompilerParams(vmem_limit_bytes=lean << 20 if lean else None),
    )(*[pltpu.with_memory_space_constraint(value, pltpu.VMEM) for value in kept], *stay, *fetched)


def project(step, x_list, w, users):
    t = x_list[0].shape[0]
    kind = pltpu.VMEM if step > 0 else jax.ShapeDtypeStruct
    outs = [kind((t, 2 * HW), jnp.bfloat16), kind((t, HW), jnp.float32)]
    kernel = functools.partial(project_kernel, step)
    scratch = [pltpu.VMEM((4, w.shape[0], HW), w.dtype), pltpu.SemaphoreType.DMA((4,))]
    kept, fetched = x_list[:step], [x_list[step], users]
    return call(kernel, outs, kept, fetched, lean=60 * step, stay=[w], scratch=scratch)


def make_mask(step, users, lengths):
    outs = [jax.ShapeDtypeStruct((users.shape[1], 2 * NX * SPAN), jnp.bfloat16)]
    kernel = functools.partial(masks_kernel, step)
    return call(kernel, outs, [], [users, lengths], lean=16 * step)[0]


def attend_early(uq, local, mask, rows):
    outs = [pltpu.VMEM(local.shape, jnp.float32)]
    return call(early_kernel, outs, [*rows, uq, local], [mask])[0]


def attend(step, x_list, uq, local, w_back, mask, rows, at=0, first=()):
    t, d = x_list[0].shape
    kernel = functools.partial(attend_kernel, step, at, len(rows))
    if step > 0:
        outs = [jax.ShapeDtypeStruct((STEPS, t, d), jnp.bfloat16)]
        kept = [*rows, w_back, x_list[0], uq, local]
        return call(kernel, outs, kept, [x_list[1], mask, *first])[0]
    outs = [pltpu.VMEM((t, d), jnp.bfloat16)]
    fetched = [*x_list, uq, local, mask]
    return call(kernel, outs, [*rows, w_back], fetched, lean=0)[0]


def body(incoming, fresh, w_uvqk, w_out, cache_kv, rows_user, cache_len):
    w_in, w_back = w_uvqk[0], w_out[0]
    evens = lax.all_gather(cache_kv[0], "ctx", axis=0, tiled=False, axis_index_groups=EVENS)
    column = [evens[:, t].reshape(SPAN, 2 * HW) for t in range(STEPS)]
    rows0 = exchange(column[0], SQUARES)
    other = lax.ppermute(column[1], "ctx", PAIR)
    near = jnp.concatenate([column[1], other], axis=0)
    rows1 = [near, lax.ppermute(near, "ctx", along_x(1))]
    rows1.append(lax.ppermute(near, "ctx", along_x(-1)))
    rows1.append(lax.ppermute(column[1], "ctx", along_x(2)))
    rows1.append(lax.ppermute(other, "ctx", along_x(-2)))
    uq, local = project(0, [incoming[0]], w_in, rows_user)
    mask0 = make_mask(0, rows_user, cache_len.T)
    mask1 = make_mask(1, rows_user, cache_len.T)
    first = attend(0, [incoming[0]], uq, local, w_back, mask0, [rows0])
    sections = lax.axis_size("pipe")
    passed = lax.ppermute(first, "pipe", [(i, i + 1) for i in range(sections - 1)])
    uq, local = project(1, [passed, fresh], w_in, rows_user)
    local = attend_early(uq, local, mask1, rows1[:-1])
    at = 2 * NX * SPAN - rows1[-1].shape[0]
    both = attend(1, [passed, fresh], uq, local, w_back, mask1, rows1[-1:], at, [first])
    return both[None]


def solution(mesh):
    in_specs = (
        P("pipe", "ctx", None),
        P("ctx", None),
        P("pipe", None, None),
        P("pipe", None, None),
        P("pipe", None, "ctx", None),
        P(None, "ctx"),
        P(),
    )
    out_specs = P("pipe", None, "ctx", None)
    return jax.shard_map(body, mesh=mesh, in_specs=in_specs, out_specs=out_specs, check_vma=False)
```

```python
import functools

import jax
import jax.numpy as jnp
from jax import lax
from jax.experimental import pallas as pl
from jax.experimental.pallas import tpu as pltpu
from jax.sharding import PartitionSpec as P


HEADS = 4
HD = 128
HW = HEADS * HD
STEPS = 2
NX = 4
NZ = 16
USERS = 4
SHARE = 16
EVENS = [[z * NX + x for z in range(p, NZ, 2)] for p in range(2) for x in range(NX)]
SQUARES = [[(2 * i + p) * NX + x for p in range(2) for x in range(NX)] for i in range(NZ // 2)]
PAIR = [(c, (c // NX + (1 if c // NX % 2 else -1)) % NZ * NX + c % NX) for c in range(NX * NZ)]
HOPS = (0, 3, 1, 2)
SPAN = SHARE * NZ // 2


def along_x(distance):
    return [(c, (c // NX) * NX + (c % NX + distance) % NX) for c in range(NX * NZ)]


def half_silu(half):
    return half + half * jnp.tanh(half)


def normalize(values):
    center = jnp.mean(values, axis=-1, keepdims=True)
    shifted = values - center
    spread = jnp.mean(shifted * shifted, axis=-1, keepdims=True)
    return shifted * lax.rsqrt(spread + 1e-06)


def dot_t(a, b):
    return lax.dot_general(a, b, (((1,), (1,)), ((), ())), preferred_element_type=jnp.float32)


def user_columns(users_ref, step):
    batch = lax.axis_size("pipe") - 1 - lax.axis_index("pipe") + step
    row = users_ref[pl.ds(batch, 1), :].astype(jnp.float32)
    square = jnp.broadcast_to(row, (row.shape[1], row.shape[1]))
    return square, square.T


def current_of(refs, step):
    if step == 0:
        return refs[0][...]
    passed, fresh = refs
    return jnp.where(lax.axis_index("pipe") == 0, fresh[...], passed[...])


def project_kernel(step, *refs):
    passed, (w_hbm, x_ref, users_ref, uq_ref, attn_ref, w_ref, arrived) = refs[:step], refs[step:]
    x_refs = (*passed, x_ref)
    fetches = [
        pltpu.make_async_copy(
            w_hbm.at[:, pl.ds(part * HW, HW)], w_ref.at[part], arrived.at[part]
        )
        for part in range(4)
    ]
    for part in (1, 2, 3, 0):
        fetches[part].start()
    normed = normalize(current_of(x_refs, step).astype(jnp.float32)).astype(jnp.bfloat16)

    def projected(part):
        fetches[part].wait()
        wide = jnp.dot(normed, w_ref[part], preferred_element_type=jnp.float32)
        return half_silu(0.5 * wide).astype(jnp.bfloat16)

    queries, keys, values = projected(1), projected(2), projected(3)
    uq_ref[:, HW:] = queries
    rows, columns = user_columns(users_ref, step)
    t = lax.broadcasted_iota(jnp.int32, rows.shape, 0)
    n = lax.broadcasted_iota(jnp.int32, rows.shape, 1)
    allowed = (rows == columns) & (n <= t)
    for h in range(HEADS):
        s = slice(h * HD, (h + 1) * HD)
        scores = dot_t(queries[:, s], keys[:, s])
        weights = jnp.where(allowed, half_silu((0.5 * HD**-0.5) * scores), 0.0)
        attn_ref[:, s] = jnp.dot(
            weights.astype(jnp.bfloat16), values[:, s], preferred_element_type=jnp.float32
        )
    uq_ref[:, :HW] = projected(0)


def fill_mask(step, users_ref, len_ref, mask_ref):
    batch = lax.axis_size("pipe") - 1 - lax.axis_index("pipe") + step
    column = lax.broadcasted_iota(jnp.int32, len_ref.shape, 1) == batch
    lengths = jnp.sum(jnp.where(column, len_ref[...], 0), axis=1, keepdims=True)
    n = lax.broadcasted_iota(jnp.int32, (8, SPAN), 1)
    base = (n // SHARE) * (2 * NX * SHARE) + n % SHARE
    bounds = [lengths[0:1]]
    for g in range(1, USERS - 1):
        bounds.append(bounds[-1] + lengths[g : g + 1])
    bounds = [jnp.broadcast_to(bound, base.shape) for bound in bounds]
    _, columns = user_columns(users_ref, step)
    for b in range(2 * NX):
        if step == 0:
            offset = b * SHARE
        else:
            x, z = lax.axis_index("ctx") % NX, lax.axis_index("ctx") // NX
            offset = (z + b) % 2 * (NX * SHARE) + (x + HOPS[b // 2]) % NX * SHARE
        position = base + offset
        owner = sum((position >= bound).astype(jnp.int32) for bound in bounds)
        row = jnp.broadcast_to(owner[:1].astype(jnp.float32), columns.shape)
        mask = (row == columns).astype(jnp.float32).astype(jnp.bfloat16)
        mask_ref[:, b * SPAN : (b + 1) * SPAN] = mask


def gathered(at, uq_ref, local_ref, mask_ref, row_refs):
    attn = []
    for h in range(HEADS):
        key_part, value_part = slice(h * HD, (h + 1) * HD), slice(HW + h * HD, HW + (h + 1) * HD)
        queries = uq_ref[:, value_part]
        total = local_ref[:, key_part]
        begin_at = at
        for row_ref in row_refs:
            size = row_ref.shape[0]
            for begin in range(0, size, 2 * SPAN):
                wide = min(2 * SPAN, size - begin)
                scores = dot_t(queries, row_ref[begin : begin + wide, key_part])
                weights = half_silu((0.5 * HD**-0.5) * scores).astype(jnp.bfloat16)
                total = total + jnp.dot(
                    weights * mask_ref[:, begin_at : begin_at + wide],
                    row_ref[begin : begin + wide, value_part],
                    preferred_element_type=jnp.float32,
                )
                begin_at += wide
        attn.append(total)
    return jnp.concatenate(attn, axis=1)


def early_kernel(*refs):
    *row_refs, uq_ref, local_ref, mask_ref, out_ref = refs
    out_ref[...] = gathered(0, uq_ref, local_ref, mask_ref, row_refs)


def attend_kernel(step, at, count, *refs):
    row_refs, w_ref, refs = refs[:count], refs[count], refs[count + 1 :]
    if step > 0:
        passed, uq_ref, local_ref, x_ref, mask_ref, *rest = refs
        x_refs = (passed, x_ref)
    else:
        x_ref, uq_ref, local_ref, users_ref, len_ref, *rest, mask_ref = refs
        x_refs = (x_ref,)
        fill_mask(step, users_ref, len_ref, mask_ref)
    whole = gathered(at, uq_ref, local_ref, mask_ref, row_refs)
    mixed = (normalize(whole) * uq_ref[:, :HW].astype(jnp.float32)).astype(jnp.bfloat16)
    result = jnp.dot(mixed, w_ref[...], preferred_element_type=jnp.float32)
    result = (result + current_of(x_refs, step).astype(jnp.float32)).astype(jnp.bfloat16)
    if step > 0:
        first_ref, out_ref = rest
        out_ref[0] = first_ref[...]
        out_ref[1] = result
    else:
        rest[0][...] = result


def exchange(block, groups):
    spread = jnp.broadcast_to(block[None], (len(groups[0]), *block.shape))
    got = lax.all_to_all(spread, "ctx", 0, 0, axis_index_groups=groups)
    return got.reshape(-1, block.shape[-1])


RESIDENT = pl.BlockSpec(memory_space=pltpu.VMEM)


def fetched_spec(value):
    return pl.BlockSpec(value.shape, lambda j: (0,) * len(value.shape))


def call(kernel, outs, kept, fetched, lean=16, stay=(), scratch=()):
    keep = not any(isinstance(out, jax.ShapeDtypeStruct) for out in outs)
    return pl.pallas_call(
        kernel,
        grid=(1,),
        in_specs=[RESIDENT for _ in kept]
        + [pl.BlockSpec(memory_space=pltpu.HBM) for _ in stay]
        + [fetched_spec(value) for value in fetched],
        out_specs=[RESIDENT if keep else fetched_spec(out) for out in outs],
        out_shape=outs,
        scratch_shapes=list(scratch),
        compiler_params=pltpu.CompilerParams(vmem_limit_bytes=lean << 20 if lean else None),
    )(*[pltpu.with_memory_space_constraint(value, pltpu.VMEM) for value in kept], *stay, *fetched)


def project(step, x_list, w, users):
    t = x_list[0].shape[0]
    kind = pltpu.VMEM if step > 0 else jax.ShapeDtypeStruct
    outs = [kind((t, 2 * HW), jnp.bfloat16), kind((t, HW), jnp.float32)]
    kernel = functools.partial(project_kernel, step)
    scratch = [pltpu.VMEM((4, w.shape[0], HW), w.dtype), pltpu.SemaphoreType.DMA((4,))]
    kept, fetched = x_list[:step], [x_list[step], users]
    return call(kernel, outs, kept, fetched, lean=60 * step, stay=[w], scratch=scratch)


def make_mask(step, users, lengths):
    outs = [jax.ShapeDtypeStruct((users.shape[1], 2 * NX * SPAN), jnp.bfloat16)]
    kernel = functools.partial(fill_mask, step)
    return call(kernel, outs, [], [users, lengths], lean=16 * step)[0]


def attend_early(uq, local, mask, rows):
    outs = [pltpu.VMEM(local.shape, jnp.float32)]
    return call(early_kernel, outs, [*rows, uq, local], [mask])[0]


def attend(step, x_list, uq, local, w_back, mask, rows, at=0, first=()):
    t, d = x_list[0].shape
    kernel = functools.partial(attend_kernel, step, at, len(rows))
    if step > 0:
        outs = [jax.ShapeDtypeStruct((STEPS, t, d), jnp.bfloat16)]
        kept = [*rows, w_back, x_list[0], uq, local]
        return call(kernel, outs, kept, [x_list[1], mask, *first])[0]
    outs = [pltpu.VMEM((t, d), jnp.bfloat16)]
    fetched = [*x_list, uq, local, *mask]
    scratch = [pltpu.VMEM((t, rows[0].shape[0]), jnp.bfloat16)]
    kept = [*rows, w_back]
    return call(kernel, outs, kept, fetched, lean=0, scratch=scratch)[0]


def body(incoming, fresh, w_uvqk, w_out, cache_kv, rows_user, cache_len):
    w_in, w_back = w_uvqk[0], w_out[0]
    evens = lax.all_gather(cache_kv[0], "ctx", axis=0, tiled=False, axis_index_groups=EVENS)
    column = [evens[:, t].reshape(SPAN, 2 * HW) for t in range(STEPS)]
    rows0 = exchange(column[0], SQUARES)
    other = lax.ppermute(column[1], "ctx", PAIR)
    near = jnp.concatenate([column[1], other], axis=0)
    mine = lax.optimization_barrier(evens)[:, 1].reshape(SPAN, 2 * HW)
    rows1 = [near, lax.ppermute(near, "ctx", along_x(1))]
    rows1.append(lax.ppermute(near, "ctx", along_x(-1)))
    rows1.append(lax.ppermute(mine, "ctx", along_x(2)))
    rows1.append(lax.ppermute(other, "ctx", along_x(-2)))
    uq, local = project(0, [incoming[0]], w_in, rows_user)
    mask1 = make_mask(1, rows_user, cache_len.T)
    first = attend(0, [incoming[0]], uq, local, w_back, (rows_user, cache_len.T), [rows0])
    sections = lax.axis_size("pipe")
    passed = lax.ppermute(first, "pipe", [(i, i + 1) for i in range(sections - 1)])
    uq, local = project(1, [passed, fresh], w_in, rows_user)
    local = attend_early(uq, local, mask1, rows1[:-1])
    at = 2 * NX * SPAN - rows1[-1].shape[0]
    both = attend(1, [passed, fresh], uq, local, w_back, mask1, rows1[-1:], at, [first])
    return both[None]


def solution(mesh):
    in_specs = (
        P("pipe", "ctx", None),
        P("ctx", None),
        P("pipe", None, None),
        P("pipe", None, None),
        P("pipe", None, "ctx", None),
        P(None, "ctx"),
        P(),
    )
    out_specs = P("pipe", None, "ctx", None)
    return jax.shard_map(body, mesh=mesh, in_specs=in_specs, out_specs=out_specs, check_vma=False)
```
